32 devices in a mesh: rep: 4 (over y, core), wide: 8 (over z, x).
Axes of the slice: x: 2, y: 2, z: 4, core: 2. Of those that a mesh axis runs over, the one named last changes fastest.
Arguments:
- shard_lost: int32 [4], replicated, may hold values from 0 to 7, as said below
- new_blocks: int32 [7], replicated, may hold values from 1 to 2, as said below
- weights: float32 [4, 1024, 1536], P('rep', 'wide'), may hold values from -3 to 3, as said below
- first_moment: float32 [4, 1024, 1536], P('rep', 'wide'), may hold values from -2 to 2, as said below
- second_moment: float32 [4, 1024, 1536], P('rep', 'wide'), may hold values from 0.05 to 1, as said below
- gradient: bfloat16 [4, 1024, 1536], P('rep', 'wide'), may hold values from -1200 to 1200
Outputs:
- new_weights: float32 [4, 2048, 1536], P('rep', 'wide')
- new_first: float32 [4, 2048, 1536], P('rep', 'wide')
- new_second: float32 [4, 2048, 1536], P('rep', 'wide')
The draws below stay inside these ranges and needn't reach their ends.
Inputs may be any that keep to these rules, and one draw needn't show every extreme that they name: `shard_lost`: the 4 values are distinct; one island lost shard 0 and another lost the last shard. `new_blocks`: the counts sum to 8; exactly one of them equals 2. All islands hold the same weights, except the 128 rows that each island lost at its lost shard, which hold arbitrary values. `first_moment`: same for the first moments. `second_moment`: same for the second moments.
All inputs are finite; a program needn't handle non-finite values.
Results may differ from the reference program's by a relative error of at most 0.0003.
Values may be sent and summed in bfloat16 or wider, within the bound.
No kernel may reach another device: no remote copies, remote signals or barrier semaphores. Data moves between devices by JAX's collectives and lax.ppermute only.
A program may use at most 64 MiB of HBM per device.

```python
import math
import jax
import jax.numpy as jnp
from jax import lax

FF = 1536
BLOCK = 128
ISLANDS = 4
OLD_SHARDS = 8
NEW_SHARDS = 7
CAP_BLK = 2
CAP_ROWS = 256
ROWS = 1024
N_WIDE = 8


def failure(key):
    base = jax.random.fold_in(key, 9001)
    middle = 1 + jax.random.permutation(jax.random.fold_in(base, 2), OLD_SHARDS - 2)
    ends = jnp.array([0, OLD_SHARDS - 1], jnp.int32)
    chosen = jnp.concatenate([ends, middle[:ISLANDS - 2].astype(jnp.int32)])
    placing = jax.random.permutation(jax.random.fold_in(base, 3), ISLANDS)
    return chosen[placing].astype(jnp.int32)


def draw_shard_lost(key, part):
    return failure(key)


def draw_new_blocks(key, part):
    extra = OLD_SHARDS - NEW_SHARDS
    biggest = CAP_BLK - 1
    others = extra - biggest
    added = jnp.zeros((NEW_SHARDS,), jnp.int32)
    if others >= 1:
        order = 1 + jax.random.permutation(jax.random.fold_in(key, 313), NEW_SHARDS - 1)
        added = added.at[0].set(1)
        added = added.at[order[0]].set(biggest)
        added = added.at[order[1:others]].set(1)
    else:
        order = jax.random.permutation(jax.random.fold_in(key, 313), NEW_SHARDS)
        added = added.at[order[0]].set(biggest)
    return (1 + added).astype(jnp.int32)


def replicated(key, common, broken):
    shards = failure(key)
    whole = jnp.broadcast_to(common[None], (ISLANDS, ROWS, FF))
    for island in range(ISLANDS):
        whole = lax.dynamic_update_slice(whole, broken[island][None], (jnp.int32(island), shards[island] * BLOCK, jnp.int32(0)))
    return whole


def draw_weights(key, part):
    first_key = jax.random.fold_in(key, 11)
    second_key = jax.random.fold_in(key, 12)
    common = jnp.clip(0.5 * jax.random.normal(first_key, (ROWS, FF), jnp.float32), -3.0, 3.0)
    broken = jax.random.uniform(second_key, (ISLANDS, BLOCK, FF), jnp.float32, -3.0, 3.0)
    return replicated(key, common, broken).astype(jnp.float32)


def draw_first_moment(key, part):
    first_key = jax.random.fold_in(key, 21)
    second_key = jax.random.fold_in(key, 22)
    common = jnp.clip(0.3 * jax.random.normal(first_key, (ROWS, FF), jnp.float32), -2.0, 2.0)
    broken = jax.random.uniform(second_key, (ISLANDS, BLOCK, FF), jnp.float32, -2.0, 2.0)
    return replicated(key, common, broken).astype(jnp.float32)


def draw_second_moment(key, part):
    first_key = jax.random.fold_in(key, 31)
    second_key = jax.random.fold_in(key, 32)
    common = jnp.exp(jax.random.uniform(first_key, (ROWS, FF), jnp.float32, math.log(0.05), 0.0))
    broken = jnp.exp(jax.random.uniform(second_key, (ISLANDS, BLOCK, FF), jnp.float32, math.log(0.05), 0.0))
    return replicated(key, common, broken).astype(jnp.float32)


def draw_gradient(key, part):
    noise_key = jax.random.fold_in(key, 41)
    row_key = jax.random.fold_in(key, 42)
    col_key = jax.random.fold_in(key, 43)
    pick_key = jax.random.fold_in(key, 45)
    ramp = jnp.power(3.0, jnp.arange(ROWS, dtype=jnp.float32) / ROWS)[None, :, None]
    ranked = jax.random.permutation(pick_key, ISLANDS)
    quiet_islands = ranked < max(1, ISLANDS // 4)
    noise = jnp.clip(jax.random.normal(noise_key, (ISLANDS, ROWS, FF), jnp.float32), -4.0, 4.0)
    rows_scale = jnp.exp(jax.random.uniform(row_key, (ISLANDS, ROWS, 1), jnp.float32, 0.0, math.log(10.0)))
    island_scale = jnp.where(quiet_islands, 1.0 / 250.0, 1.0)
    cols_scale = jnp.exp(jax.random.uniform(col_key, (1, 1, FF), jnp.float32, 0.0, math.log(10.0)))
    scaled = noise * rows_scale * cols_scale * ramp * island_scale.astype(jnp.float32)[:, None, None]
    return scaled.astype(jnp.bfloat16)


def setup_inputs(seed: int = 0) -> dict:
    key_of = jax.random.split(jax.random.key(seed), 7)
    shard_lost = draw_shard_lost(jax.random.fold_in(key_of[6], 71), 0)
    new_blocks = draw_new_blocks(jax.random.fold_in(key_of[6], 71), 0)
    weights = draw_weights(jax.random.fold_in(key_of[6], 71), 0)
    first_moment = draw_first_moment(jax.random.fold_in(key_of[6], 71), 0)
    second_moment = draw_second_moment(jax.random.fold_in(key_of[6], 71), 0)
    gradient = draw_gradient(jax.random.fold_in(key_of[6], 71), 0)
    return {"shard_lost": shard_lost, "new_blocks": new_blocks, "weights": weights, "first_moment": first_moment, "second_moment": second_moment, "gradient": gradient}


beta_first = 0.9
beta_second = 0.95
bias_first = 1.0 - 0.9 ** 20
bias_second = 1.0 - 0.95 ** 20
learn_rate = 0.01
weight_decay = 0.1
eps_adam = 1e-08

def adam_update(params, moment_one, moment_two, grad_in, factor):
    clipped = grad_in.astype(jnp.float32) * factor
    one_new = beta_first * moment_one + (1.0 - beta_first) * clipped
    two_new = beta_second * moment_two + (1.0 - beta_second) * clipped * clipped
    step_dir = one_new / bias_first / (jnp.sqrt(two_new / bias_second) + eps_adam)
    params_new = params - learn_rate * (step_dir + weight_decay * params)
    return (params_new, one_new, two_new)

def reference(shard_lost, new_blocks, weights, first_moment, second_moment, gradient):

    def recover(array):
        pieces = []
        for island in range(ISLANDS):
            lost_row = (shard_lost[island] * BLOCK).astype(jnp.int32)
            healthy = array[(island + 1) % ISLANDS]
            pieces.append(lax.dynamic_slice_in_dim(healthy, lost_row, BLOCK, 0))
        result = array
        for island in range(ISLANDS):
            lost_row = (shard_lost[island] * BLOCK).astype(jnp.int32)
            result = lax.dynamic_update_slice(result, pieces[island][None], (jnp.int32(island), lost_row, jnp.int32(0)))
        return result
    counts = jnp.concatenate([new_blocks, jnp.zeros((N_WIDE // 8,), jnp.int32)])
    starts = jnp.cumsum(counts) - counts
    slots = jnp.arange(N_WIDE * CAP_ROWS, dtype=jnp.int32)
    owner = slots // CAP_ROWS
    within = slots % CAP_ROWS
    valid = within < counts[owner] * BLOCK
    source_rows = jnp.minimum(starts[owner] * BLOCK + within, ROWS - 1).astype(jnp.int32)
    limit = 0.5 * math.sqrt(ROWS * FF)

    def per_island(items):
        params, moment_one, moment_two, grad_in = items
        norm_sum = jnp.sum(jnp.square(grad_in.astype(jnp.float32)))
        factor = jnp.minimum(1.0, limit / (jnp.sqrt(norm_sum) + 1e-06))
        updated = adam_update(params, moment_one, moment_two, grad_in, factor)
        return tuple((jnp.where(valid[:, None], jnp.take(item, source_rows, axis=0), 0.0) for item in updated))
    outputs = lax.map(per_island, (recover(weights), recover(first_moment), recover(second_moment), gradient))
    return (outputs[0], outputs[1], outputs[2])
```

```python
import functools
import math

import jax
import jax.numpy as jnp
from jax import lax
from jax.experimental import pallas as pl
from jax.experimental.pallas import tpu as pltpu
from jax.sharding import PartitionSpec as P


beta_first = 0.9
beta_second = 0.95
bias_first = 1.0 - 0.9**20
bias_second = 1.0 - 0.95**20
learn_rate = 0.01
weight_decay = 0.1
eps_adam = 1e-08

code_power = (14.0, 14.0, 24.0)
code_offset = (2.0**-16, 2.0**-16, 0.0)
code_shift = (100.0, 100.0, 40.0)
code_signed = (True, True, False)

GROUP = 4
STREAMS = (((0, 1), 4), ((2,), 2))
PREP_MIB = 53.4
TILE_ROWS = 16
TILE_COLS = 512


def shifted(value, axis, steps):
    count = lax.axis_size(axis)
    initial, last = (max(0, -steps), min(count, count - steps))
    return lax.ppermute(value, axis, [(source, source + steps) for source in range(initial, last)])


def swapped(value, axis, bit):
    count = lax.axis_size(axis)
    return lax.ppermute(value, axis, [(source, source ^ bit) for source in range(count)])


def encode(value, index):
    log = jnp.log2(jnp.abs(value) + code_offset[index])
    coded = jnp.exp2(log * code_power[index] + code_shift[index])
    if code_signed[index]:
        coded = jnp.where(value < 0.0, -coded, coded)
    return coded.astype(jnp.bfloat16)


def decode(coded, index):
    wide = coded.astype(jnp.float32)
    size = jnp.abs(wide) if code_signed[index] else wide
    log = jnp.log2(size) * (1.0 / code_power[index]) - code_shift[index] / code_power[index]
    found = jnp.exp2(log) - code_offset[index]
    if code_signed[index]:
        found = jnp.where(wide < 0.0, -found, found)
    return found


def adam_update(params, moment_one, moment_two, grad_in, factor):
    clipped = grad_in.astype(jnp.float32) * factor
    one_new = beta_first * moment_one + (1.0 - beta_first) * clipped
    two_new = beta_second * moment_two + (1.0 - beta_second) * clipped * clipped
    step_dir = one_new * (1.0 / bias_first) / (jnp.sqrt(two_new * (1.0 / bias_second)) + eps_adam)
    params_new = params - learn_rate * (step_dir + weight_decay * params)
    return (params_new, one_new, two_new)


def hbm_spec():
    return pl.BlockSpec(memory_space=pltpu.HBM)


def vmem_spec():
    return pl.BlockSpec(memory_space=pltpu.VMEM)


def params_of(mebibytes):
    return pltpu.CompilerParams(vmem_limit_bytes=int(mebibytes * 2**20))


def sent_rows(share, rows):
    part = rows // GROUP
    first = lax.rem(lax.axis_index("rep"), share)
    for step in range(GROUP // share):
        yield pl.multiple_of((first + share * step) * part, part)


def plan(table_ref, skipped):
    shard = lax.axis_index("wide")
    first, count = (jnp.int32(0), jnp.int32(0))
    for index in range(table_ref.shape[0] - skipped):
        here = table_ref[skipped + index]
        first = first + jnp.where(index < shard, here, 0)
        count = count + jnp.where(index == shard, here, 0)
    return (shard, first, count)


def prep_kernel(slots, distances, islands, table_hbm, grad_hbm, *refs):
    own, (sum_ref, plan_ref), refs = (refs[:3], refs[3:5], refs[5:])
    coded, refs = (refs[: len(STREAMS)], refs[len(STREAMS) :])
    outs, (table_ref, grad_ref, held, zeros, table_sem, grad_sems, sems, zero_sems) = (refs[:3], refs[3:])
    rows, cols = grad_ref.shape
    part = rows // GROUP

    def grad_copy(step):
        here = pl.ds(step * part, part)
        return pltpu.make_async_copy(grad_hbm.at[here], grad_ref.at[here], grad_sems.at[step])

    def zero_copy(slot, index):
        return pltpu.make_async_copy(zeros, outs[index].at[pl.ds(slot * rows, rows)], zero_sems.at[slot, index])

    table_copy = pltpu.make_async_copy(table_hbm, table_ref, table_sem)
    copies = []
    for arrays, share in STREAMS:
        for index in arrays:
            for start in sent_rows(share, rows):
                place = len(copies)
                copies.append(pltpu.make_async_copy(own[index].at[pl.ds(start, part)], held.at[place], sems.at[place]))
    table_copy.start()
    for step in range(GROUP):
        grad_copy(step).start()
    for copy in copies:
        copy.start()
    zeros[...] = jnp.zeros_like(zeros)
    table_copy.wait()
    shard, first, count = plan(table_ref, islands)
    for slot in range(slots):

        @pl.when(slot >= count)
        def _():
            for index in range(3):
                zero_copy(slot, index).start()

    broken = table_ref[lax.axis_index("rep")] == shard
    facts = [broken.astype(jnp.int32)]
    for distance in range(distances + 1):
        slot = shard + distance - first
        facts.append(jnp.where(jnp.logical_and(slot >= 0, slot < count), slot, -1))
    line = lax.broadcasted_iota(jnp.int32, plan_ref.shape, 0)
    found = jnp.zeros(plan_ref.shape, jnp.int32)
    for index, fact in enumerate(facts):
        found = jnp.where(line == index, fact, found)
    plan_ref[...] = found

    total = jnp.zeros((16, 128), jnp.float32)
    for step in range(GROUP):
        grad_copy(step).wait()
        for row in range(step * part, (step + 1) * part, 16):
            for col in range(0, cols, 128):
                piece = grad_ref[row : row + 16, col : col + 128].astype(jnp.float32)
                total = total + piece * piece
    sum_ref[...] = total[:8] + total[8:]
    place = 0
    for (arrays, share), out in zip(STREAMS, coded):
        line = 0
        for index in arrays:
            for _ in range(GROUP // share):
                copies[place].wait()
                out[line : line + part] = encode(held[place], index)
                place, line = (place + 1, line + part)
    for slot in range(slots):

        @pl.when(slot >= count)
        def _():
            for index in range(3):
                zero_copy(slot, index).wait()


def prep(tables, islands, grad, own, slots, distances):
    rows, cols = grad.shape
    part = rows // GROUP
    lines = [len(arrays) * (GROUP // share) for arrays, share in STREAMS]
    return pl.pallas_call(
        functools.partial(prep_kernel, slots, distances, islands),
        out_shape=[jax.ShapeDtypeStruct((8, 128), jnp.float32), jax.ShapeDtypeStruct((8, 128), jnp.int32)]
        + [jax.ShapeDtypeStruct((count * part, cols), jnp.bfloat16) for count in lines]
        + [jax.ShapeDtypeStruct((slots * rows, cols), jnp.float32)] * 3,
        in_specs=[hbm_spec()] * 5,
        out_specs=[vmem_spec()] * (2 + len(lines)) + [hbm_spec()] * 3,
        scratch_shapes=[
            pltpu.SMEM(tables.shape, jnp.int32),
            pltpu.VMEM((rows, cols), jnp.bfloat16),
            pltpu.VMEM((sum(lines), part, cols), jnp.float32),
            pltpu.VMEM((rows, cols), jnp.float32),
            pltpu.SemaphoreType.DMA,
            pltpu.SemaphoreType.DMA((GROUP,)),
            pltpu.SemaphoreType.DMA((sum(lines),)),
            pltpu.SemaphoreType.DMA((slots, 3)),
        ],
        cost_estimate=pl.CostEstimate(flops=4 * grad.size, bytes_accessed=20 * grad.size, transcendentals=grad.size),
        compiler_params=params_of(PREP_MIB),
        name="prep",
    )(tables, grad, *own)


def pack_kernel(plan_ref, *refs):
    peer, refs = (refs[:3], refs[3:])
    coded, outs = (refs[: len(STREAMS)], refs[len(STREAMS) :])
    rows = peer[0].shape[0]
    part = rows // GROUP
    broken = plan_ref[0:1, 0:1] != 0
    for (arrays, share), own, out in zip(STREAMS, coded, outs):
        line = 0
        for index in arrays:
            for start in sent_rows(share, rows):
                here = slice(line, line + part)
                fixed = encode(peer[index][pl.ds(start, part)], index)
                out[here] = jnp.where(broken, fixed.astype(jnp.float32), own[here].astype(jnp.float32)).astype(jnp.bfloat16)
                line += part


def pack(table, peer, coded):
    return pl.pallas_call(
        pack_kernel,
        out_shape=[jax.ShapeDtypeStruct(piece.shape, piece.dtype) for piece in coded],
        in_specs=[vmem_spec()] * (4 + len(coded)),
        out_specs=[vmem_spec()] * len(coded),
        cost_estimate=pl.CostEstimate(flops=8 * peer[0].size, bytes_accessed=8 * peer[0].size, transcendentals=peer[0].size),
        compiler_params=params_of(8),
        name="pack",
    )(table, *peer, *coded)


def last_kernel(limit, distances, plan_ref, total_ref, grad_ref, *refs):
    own, peer, refs = (refs[:3], refs[3:6], refs[6:])
    arrived = []
    for _ in range(distances):
        coded = []
        for _, share in STREAMS:
            coded.append(refs[:share])
            refs = refs[share:]
        arrived.append((coded, refs[0]))
        refs = refs[1:]
    outs, (ready, sems) = (refs[3:6], refs[6:])
    rows, cols = ready.shape[2:]
    part = rows // GROUP
    me = lax.rem(lax.axis_index("rep"), GROUP)
    place = [jnp.max(plan_ref[1 + distance : 2 + distance, :]) for distance in range(distances + 1)]
    norm_sum = jnp.sum(total_ref[...], keepdims=True)
    factor = jnp.minimum(1.0, limit / (jnp.sqrt(norm_sum) + 1e-06))

    def slot_of(distance):
        return (jnp.maximum(place[distance], 0), place[distance] >= 0)

    def quarter_of(distance, turn):
        return turn if distance == 0 else jnp.bitwise_xor(me, turn)

    def out_copy(distance, turn, index):
        start = slot_of(distance)[0] * rows + quarter_of(distance, turn) * part
        target = pl.ds(pl.multiple_of(start, part), part)
        source = ready.at[distance, index, pl.ds(turn * part, part)]
        return pltpu.make_async_copy(source, outs[index].at[target], sems.at[distance, turn, index])

    def finish(distance, turn, load):
        for row in range(0, part, TILE_ROWS):
            here = slice(turn * part + row, turn * part + row + TILE_ROWS)
            for col in range(0, cols, TILE_COLS):
                lanes = slice(col, col + TILE_COLS)
                fresh = adam_update(*load(row, lanes), factor)
                for index in range(3):
                    ready[distance, index, here, lanes] = fresh[index]
        for index in range(3):
            out_copy(distance, turn, index).start()

    @pl.when(slot_of(0)[1])
    def _():
        broken = plan_ref[0:1, 0:1] != 0
        for turn in range(GROUP):

            def load(row, lanes):
                here = slice(turn * part + row, turn * part + row + TILE_ROWS)
                states = [jnp.where(broken, peer[index][here, lanes], own[index][here, lanes]) for index in range(3)]
                return (*states, grad_ref[here, lanes])

            finish(0, turn, load)

    for distance, (coded, grad) in enumerate(arrived, 1):

        @pl.when(slot_of(distance)[1])
        def _():
            for turn in range(GROUP):
                quarter = quarter_of(distance, turn)

                def load(row, lanes):
                    states = [None] * 3
                    for (arrays, share), found in zip(STREAMS, coded):
                        for line, index in enumerate(arrays):
                            start = (line * (GROUP // share) + lax.div(quarter, share)) * part + row
                            here = pl.ds(pl.multiple_of(start, TILE_ROWS), TILE_ROWS)
                            states[index] = decode(found[turn % share][here, lanes], index)
                    return (*states, grad[pl.ds(pl.multiple_of(quarter * part + row, TILE_ROWS), TILE_ROWS), lanes])

                finish(distance, turn, load)

    for distance in range(distances + 1):

        @pl.when(slot_of(distance)[1])
        def _():
            for turn in range(GROUP):
                for index in range(3):
                    out_copy(distance, turn, index).wait()


def last(table, total, grad, own, peer, arrived, outs, limit):
    rows, cols = grad.shape
    distances = len(arrived)
    flat = [piece for pieces in arrived for piece in pieces]
    fixed = 9 + len(flat)
    return pl.pallas_call(
        functools.partial(last_kernel, limit, distances),
        out_shape=[jax.ShapeDtypeStruct(out.shape, out.dtype) for out in outs],
        in_specs=[vmem_spec()] * fixed + [hbm_spec()] * 3,
        out_specs=[hbm_spec()] * 3,
        input_output_aliases={fixed + index: index for index in range(3)},
        scratch_shapes=[
            pltpu.VMEM((distances + 1, 3, rows, cols), jnp.float32),
            pltpu.SemaphoreType.DMA((distances + 1, GROUP, 3)),
        ],
        cost_estimate=pl.CostEstimate(
            flops=40 * rows * cols, bytes_accessed=32 * rows * cols, transcendentals=8 * rows * cols
        ),
        compiler_params=params_of(10 + 6 * distances),
        name="last",
    )(table, total, grad, *own, *peer, *flat, *outs)


def steps_of(count):
    return (count - 1).bit_length()


def program(shard_lost, new_blocks, weights, first_moment, second_moment, gradient):
    shards = lax.axis_size("wide")
    max_shift = shards // 8
    slots = 1 + min(2, max_shift)
    rows, cols = gradient.shape[1:]
    limit = 0.5 * math.sqrt(rows * shards * cols)
    own = [weights[0], first_moment[0], second_moment[0]]
    grad = gradient[0]

    tables = jnp.concatenate([shard_lost, new_blocks])
    peer = [swapped(value, "rep", 1) for value in own]
    total, table, *made = prep(tables, shard_lost.shape[0], grad, own, slots, max_shift)
    coded, outs = (made[: len(STREAMS)], made[len(STREAMS) :])
    packed = pack(table, peer, coded)
    for step in range(steps_of(shards)):
        total = total + swapped(total, "wide", 1 << step)

    arrived = []
    for distance in range(1, max_shift + 1):
        moved = shifted(grad, "wide", -distance)
        found = []
        for stream, (_, share) in enumerate(STREAMS):
            held = [shifted(packed[stream], "wide", -distance)]
            bit = share // 2
            while bit:
                more = [swapped(piece, "rep", bit) for piece in held]
                held = [piece for pair in zip(held, more) for piece in pair]
                bit //= 2
            found.extend(held)
        arrived.append(found + [moved])

    outs = last(table, total, grad, own, peer, arrived, outs, limit)
    return tuple(out[None] for out in outs)


def solution(mesh):
    return jax.shard_map(
        program,
        mesh=mesh,
        in_specs=(
            P(),
            P(),
            P("rep", "wide", None),
            P("rep", "wide", None),
            P("rep", "wide", None),
            P("rep", "wide", None),
        ),
        out_specs=(P("rep", "wide", None), P("rep", "wide", None), P("rep", "wide", None)),
        check_vma=False,
    )
```

```python
import functools
import math

import jax
import jax.numpy as jnp
from jax import lax
from jax.experimental import pallas as pl
from jax.experimental.pallas import tpu as pltpu
from jax.sharding import PartitionSpec as P


beta_first = 0.9
beta_second = 0.95
bias_first = 1.0 - 0.9**20
bias_second = 1.0 - 0.95**20
learn_rate = 0.01
weight_decay = 0.1
eps_adam = 1e-08

code_power = (14.0, 14.0, 24.0)
code_offset = (2.0**-16, 2.0**-16, 0.0)
code_shift = (100.0, 100.0, 40.0)
code_signed = (True, True, False)

GROUP = 4
STREAMS = (((0, 1), 4), ((2,), 2))
PREP_MIB = 53.4
TILE_ROWS = 16
TILE_COLS = 256


def shifted(value, axis, steps):
    count = lax.axis_size(axis)
    initial, last = (max(0, -steps), min(count, count - steps))
    return lax.ppermute(value, axis, [(source, source + steps) for source in range(initial, last)])


def swapped(value, axis, bit):
    count = lax.axis_size(axis)
    return lax.ppermute(value, axis, [(source, source ^ bit) for source in range(count)])


def encode(value, index):
    log = jnp.log2(jnp.abs(value) + code_offset[index])
    coded = jnp.exp2(log * code_power[index] + code_shift[index])
    if code_signed[index]:
        coded = jnp.where(value < 0.0, -coded, coded)
    return coded.astype(jnp.bfloat16)


def decode(coded, index):
    wide = coded.astype(jnp.float32)
    size = jnp.abs(wide) if code_signed[index] else wide
    log = jnp.log2(size) * (1.0 / code_power[index]) - code_shift[index] / code_power[index]
    found = jnp.exp2(log) - code_offset[index]
    if code_signed[index]:
        found = jnp.where(wide < 0.0, -found, found)
    return found


def adam_update(params, moment_one, moment_two, grad_in, factor):
    clipped = grad_in.astype(jnp.float32) * factor
    one_new = beta_first * moment_one + (1.0 - beta_first) * clipped
    two_new = beta_second * moment_two + (1.0 - beta_second) * clipped * clipped
    step_dir = one_new * (1.0 / bias_first) / (jnp.sqrt(two_new * (1.0 / bias_second)) + eps_adam)
    params_new = params - learn_rate * (step_dir + weight_decay * params)
    return (params_new, one_new, two_new)


def hbm_spec():
    return pl.BlockSpec(memory_space=pltpu.HBM)


def vmem_spec():
    return pl.BlockSpec(memory_space=pltpu.VMEM)


def params_of(mebibytes):
    return pltpu.CompilerParams(vmem_limit_bytes=int(mebibytes * 2**20))


def sent_rows(share, rows):
    part = rows // GROUP
    first = lax.rem(lax.axis_index("rep"), share)
    for step in range(GROUP // share):
        yield pl.multiple_of((first + share * step) * part, part)


def plan(blocks_ref):
    shard = lax.axis_index("wide")
    first, count = (jnp.int32(0), jnp.int32(0))
    for index in range(blocks_ref.shape[0]):
        here = blocks_ref[index]
        first = first + jnp.where(index < shard, here, 0)
        count = count + jnp.where(index == shard, here, 0)
    return (shard, first, count)


def prep_kernel(slots, distances, lost_hbm, blocks_hbm, grad_hbm, *refs):
    own, (sum_ref, plan_ref), refs = (refs[:3], refs[3:5], refs[5:])
    coded, refs = (refs[: len(STREAMS)], refs[len(STREAMS) :])
    outs, (lost_ref, blocks_ref, grad_ref, held, zeros, table_sems, grad_sems, sems, zero_sems) = (refs[:3], refs[3:])
    rows, cols = grad_ref.shape
    part = rows // GROUP

    def grad_copy(step):
        here = pl.ds(step * part, part)
        return pltpu.make_async_copy(grad_hbm.at[here], grad_ref.at[here], grad_sems.at[step])

    def zero_copy(slot, index):
        return pltpu.make_async_copy(zeros, outs[index].at[pl.ds(slot * rows, rows)], zero_sems.at[slot, index])

    tables = [
        pltpu.make_async_copy(blocks_hbm, blocks_ref, table_sems.at[0]),
        pltpu.make_async_copy(lost_hbm, lost_ref, table_sems.at[1]),
    ]
    copies = []
    for arrays, share in STREAMS:
        for index in arrays:
            for start in sent_rows(share, rows):
                place = len(copies)
                copies.append(pltpu.make_async_copy(own[index].at[pl.ds(start, part)], held.at[place], sems.at[place]))
    for copy in tables:
        copy.start()
    for step in range(GROUP):
        grad_copy(step).start()
    for copy in copies:
        copy.start()
    zeros[...] = jnp.zeros_like(zeros)
    for copy in tables:
        copy.wait()
    shard, first, count = plan(blocks_ref)
    for slot in range(slots):

        @pl.when(slot >= count)
        def _():
            for index in range(3):
                zero_copy(slot, index).start()

    broken = lost_ref[lax.axis_index("rep")] == shard
    facts = [broken.astype(jnp.int32)]
    for distance in range(distances + 1):
        slot = shard + distance - first
        facts.append(jnp.where(jnp.logical_and(slot >= 0, slot < count), slot, -1))
    line = lax.broadcasted_iota(jnp.int32, plan_ref.shape, 0)
    table = jnp.zeros(plan_ref.shape, jnp.int32)
    for index, fact in enumerate(facts):
        table = jnp.where(line == index, fact, table)
    plan_ref[...] = table

    total = jnp.zeros((16, 128), jnp.float32)
    for step in range(GROUP):
        grad_copy(step).wait()
        for row in range(step * part, (step + 1) * part, 16):
            for col in range(0, cols, 128):
                piece = grad_ref[row : row + 16, col : col + 128].astype(jnp.float32)
                total = total + piece * piece
    sum_ref[...] = total[:8] + total[8:]
    place = 0
    for (arrays, share), out in zip(STREAMS, coded):
        line = 0
        for index in arrays:
            for _ in range(GROUP // share):
                copies[place].wait()
                out[line : line + part] = encode(held[place], index)
                place, line = (place + 1, line + part)
    for slot in range(slots):

        @pl.when(slot >= count)
        def _():
            for index in range(3):
                zero_copy(slot, index).wait()


def prep(shard_lost, new_blocks, grad, own, slots, distances):
    rows, cols = grad.shape
    part = rows // GROUP
    lines = [len(arrays) * (GROUP // share) for arrays, share in STREAMS]
    return pl.pallas_call(
        functools.partial(prep_kernel, slots, distances),
        out_shape=[jax.ShapeDtypeStruct((8, 128), jnp.float32), jax.ShapeDtypeStruct((8, 128), jnp.int32)]
        + [jax.ShapeDtypeStruct((count * part, cols), jnp.bfloat16) for count in lines]
        + [jax.ShapeDtypeStruct((slots * rows, cols), jnp.float32)] * 3,
        in_specs=[hbm_spec()] * 6,
        out_specs=[vmem_spec()] * (2 + len(lines)) + [hbm_spec()] * 3,
        scratch_shapes=[
            pltpu.SMEM(shard_lost.shape, jnp.int32),
            pltpu.SMEM(new_blocks.shape, jnp.int32),
            pltpu.VMEM((rows, cols), jnp.bfloat16),
            pltpu.VMEM((sum(lines), part, cols), jnp.float32),
            pltpu.VMEM((rows, cols), jnp.float32),
            pltpu.SemaphoreType.DMA((2,)),
            pltpu.SemaphoreType.DMA((GROUP,)),
            pltpu.SemaphoreType.DMA((sum(lines),)),
            pltpu.SemaphoreType.DMA((slots, 3)),
        ],
        cost_estimate=pl.CostEstimate(flops=4 * grad.size, bytes_accessed=20 * grad.size, transcendentals=grad.size),
        compiler_params=params_of(PREP_MIB),
        name="prep",
    )(shard_lost, new_blocks, grad, *own)


def pack_kernel(plan_ref, *refs):
    peer, refs = (refs[:3], refs[3:])
    coded, outs = (refs[: len(STREAMS)], refs[len(STREAMS) :])
    rows = peer[0].shape[0]
    part = rows // GROUP
    broken = plan_ref[0:1, 0:1] != 0
    for (arrays, share), own, out in zip(STREAMS, coded, outs):
        line = 0
        for index in arrays:
            for start in sent_rows(share, rows):
                here = slice(line, line + part)
                fixed = encode(peer[index][pl.ds(start, part)], index)
                out[here] = jnp.where(broken, fixed.astype(jnp.float32), own[here].astype(jnp.float32)).astype(jnp.bfloat16)
                line += part


def pack(table, peer, coded):
    return pl.pallas_call(
        pack_kernel,
        out_shape=[jax.ShapeDtypeStruct(piece.shape, piece.dtype) for piece in coded],
        in_specs=[vmem_spec()] * (4 + len(coded)),
        out_specs=[vmem_spec()] * len(coded),
        cost_estimate=pl.CostEstimate(flops=8 * peer[0].size, bytes_accessed=8 * peer[0].size, transcendentals=peer[0].size),
        compiler_params=params_of(8),
        name="pack",
    )(table, *peer, *coded)


def last_kernel(limit, distances, plan_ref, total_ref, grad_ref, *refs):
    own, peer, refs = (refs[:3], refs[3:6], refs[6:])
    arrived = []
    for _ in range(distances):
        coded = []
        for _, share in STREAMS:
            coded.append(refs[:share])
            refs = refs[share:]
        arrived.append((coded, refs[0]))
        refs = refs[1:]
    outs, (ready, sems) = (refs[3:6], refs[6:])
    rows, cols = ready.shape[2:]
    part = rows // GROUP
    me = lax.rem(lax.axis_index("rep"), GROUP)
    place = [jnp.max(plan_ref[1 + distance : 2 + distance, :]) for distance in range(distances + 1)]
    norm_sum = jnp.sum(total_ref[...], keepdims=True)
    factor = jnp.minimum(1.0, limit / (jnp.sqrt(norm_sum) + 1e-06))

    def slot_of(distance):
        return (jnp.maximum(place[distance], 0), place[distance] >= 0)

    def quarter_of(distance, turn):
        return turn if distance == 0 else jnp.bitwise_xor(me, turn)

    def out_copy(distance, turn, index):
        start = slot_of(distance)[0] * rows + quarter_of(distance, turn) * part
        target = pl.ds(pl.multiple_of(start, part), part)
        source = ready.at[distance, index, pl.ds(turn * part, part)]
        return pltpu.make_async_copy(source, outs[index].at[target], sems.at[distance, turn, index])

    def finish(distance, turn, load):
        for row in range(0, part, TILE_ROWS):
            here = slice(turn * part + row, turn * part + row + TILE_ROWS)
            for col in range(0, cols, TILE_COLS):
                lanes = slice(col, col + TILE_COLS)
                fresh = adam_update(*load(row, lanes), factor)
                for index in range(3):
                    ready[distance, index, here, lanes] = fresh[index]
        for index in range(3):
            out_copy(distance, turn, index).start()

    @pl.when(slot_of(0)[1])
    def _():
        broken = plan_ref[0:1, 0:1] != 0
        for turn in range(GROUP):

            def load(row, lanes):
                here = slice(turn * part + row, turn * part + row + TILE_ROWS)
                states = [jnp.where(broken, peer[index][here, lanes], own[index][here, lanes]) for index in range(3)]
                return (*states, grad_ref[here, lanes])

            finish(0, turn, load)

    for distance, (coded, grad) in enumerate(arrived, 1):

        @pl.when(slot_of(distance)[1])
        def _():
            for turn in range(GROUP):
                quarter = quarter_of(distance, turn)

                def load(row, lanes):
                    states = [None] * 3
                    for (arrays, share), found in zip(STREAMS, coded):
                        for line, index in enumerate(arrays):
                            start = (line * (GROUP // share) + lax.div(quarter, share)) * part + row
                            here = pl.ds(pl.multiple_of(start, TILE_ROWS), TILE_ROWS)
                            states[index] = decode(found[turn % share][here, lanes], index)
                    return (*states, grad[pl.ds(pl.multiple_of(quarter * part + row, TILE_ROWS), TILE_ROWS), lanes])

                finish(distance, turn, load)

    for distance in range(distances + 1):

        @pl.when(slot_of(distance)[1])
        def _():
            for turn in range(GROUP):
                for index in range(3):
                    out_copy(distance, turn, index).wait()


def last(table, total, grad, own, peer, arrived, outs, limit):
    rows, cols = grad.shape
    distances = len(arrived)
    flat = [piece for pieces in arrived for piece in pieces]
    fixed = 9 + len(flat)
    return pl.pallas_call(
        functools.partial(last_kernel, limit, distances),
        out_shape=[jax.ShapeDtypeStruct(out.shape, out.dtype) for out in outs],
        in_specs=[vmem_spec()] * fixed + [hbm_spec()] * 3,
        out_specs=[hbm_spec()] * 3,
        input_output_aliases={fixed + index: index for index in range(3)},
        scratch_shapes=[
            pltpu.VMEM((distances + 1, 3, rows, cols), jnp.float32),
            pltpu.SemaphoreType.DMA((distances + 1, GROUP, 3)),
        ],
        cost_estimate=pl.CostEstimate(
            flops=40 * rows * cols, bytes_accessed=32 * rows * cols, transcendentals=8 * rows * cols
        ),
        compiler_params=params_of(10 + 6 * distances),
        name="last",
    )(table, total, grad, *own, *peer, *flat, *outs)


def steps_of(count):
    return (count - 1).bit_length()


def program(shard_lost, new_blocks, weights, first_moment, second_moment, gradient):
    shards = lax.axis_size("wide")
    max_shift = shards // 8
    slots = 1 + min(2, max_shift)
    rows, cols = gradient.shape[1:]
    limit = 0.5 * math.sqrt(rows * shards * cols)
    own = [weights[0], first_moment[0], second_moment[0]]
    grad = gradient[0]

    peer = [swapped(value, "rep", 1) for value in own]
    total, table, *made = prep(shard_lost, new_blocks, grad, own, slots, max_shift)
    coded, outs = (made[: len(STREAMS)], made[len(STREAMS) :])
    packed = pack(table, peer, coded)
    for step in range(steps_of(shards)):
        total = total + swapped(total, "wide", 1 << step)

    arrived = []
    for distance in range(1, max_shift + 1):
        moved = shifted(grad, "wide", -distance)
        found = []
        for stream, (_, share) in enumerate(STREAMS):
            held = [shifted(packed[stream], "wide", -distance)]
            bit = share // 2
            while bit:
                more = [swapped(piece, "rep", bit) for piece in held]
                held = [piece for pair in zip(held, more) for piece in pair]
                bit //= 2
            found.extend(held)
        arrived.append(found + [moved])

    outs = last(table, total, grad, own, peer, arrived, outs, limit)
    return tuple(out[None] for out in outs)


def solution(mesh):
    return jax.shard_map(
        program,
        mesh=mesh,
        in_specs=(
            P(),
            P(),
            P("rep", "wide", None),
            P("rep", "wide", None),
            P("rep", "wide", None),
            P("rep", "wide", None),
        ),
        out_specs=(P("rep", "wide", None), P("rep", "wide", None), P("rep", "wide", None)),
        check_vma=False,
    )
```
